32 devices in a mesh: groups: 2 (over x), ctx: 16 (over z, y, core).
Axes of the slice: x: 2, y: 2, z: 4, core: 2. Of those that a mesh axis runs over, the one named last changes fastest.
Arguments:
- queries: bfloat16 [4096, 2048], P(('groups', 'ctx')), parts along dimension 0, may hold values from -6 to 6
- keys: bfloat16 [4096, 2048], P(('groups', 'ctx')), parts along dimension 0, may hold values from -6 to 6
- values: bfloat16 [4096, 2048], P(('groups', 'ctx')), parts along dimension 0, may hold values from -6 to 6
- out_grad: bfloat16 [4096, 2048], P(('groups', 'ctx')), parts along dimension 0, may hold values from -6 to 6
- conv_weight: float32 [8, 16], replicated, may hold values from -2 to 2
Outputs:
- dq: bfloat16 [4096, 2048], P(('groups', 'ctx')), parts along dimension 0
- dk: bfloat16 [4096, 2048], P(('groups', 'ctx')), parts along dimension 0
- dv: bfloat16 [4096, 2048], P(('groups', 'ctx')), parts along dimension 0
- dconv: float32 [16, 16], P('groups'), parts along dimension 0
The draws below stay inside these ranges and needn't reach their ends.
There are 2 independent parts, one for each index of `groups`. The reference program is written for one: setup_inputs(seed, part) draws one part's arguments, and reference() takes and returns one part's arrays. A program takes and returns all parts, laid end to end along the dimension named above; an argument that names none is the same for every part. Nothing has to cross between parts.
All inputs are finite; a program needn't handle non-finite values.
Results may differ from the reference program's by a relative error of at most 0.024.
Values may be sent and summed in bfloat16 or wider, within the bound.
A program may use at most 128 MiB of HBM per device.

```python
import jax
import jax.numpy as jnp
from jax import lax

HEADS = 16
HEAD_DIM = 128
STRIDE = 8
TOK_DEV = 128
MEM_ROWS = 16
TOKENS = 2048
WIDTH = 2048
N_CTX = 16


def draw_queries(key, part):
    fresh_key = jax.random.fold_in(key, 11)
    return jnp.clip(jax.random.normal(fresh_key, (TOKENS, WIDTH), jnp.float32), -6.0, 6.0).astype(jnp.bfloat16)


def draw_keys(key, part):
    fresh_key = jax.random.fold_in(key, 13)
    return jnp.clip(jax.random.normal(fresh_key, (TOKENS, WIDTH), jnp.float32), -6.0, 6.0).astype(jnp.bfloat16)


def steps_of(stream_key, dims, cuts, least, largest):
    gain = 1.0
    for dim, parts in cuts:
        draws = jax.random.uniform(jax.random.fold_in(jax.random.fold_in(stream_key, 6), dim), (parts,), jnp.float32, least / len(cuts), largest / len(cuts))
        gain = gain * jnp.repeat(jnp.exp(draws), dims[dim] // parts).reshape((-1,) + (1,) * (len(dims) - 1 - dim))
    return gain


def noise(rng, extent, spread, limit, cuts=(), kind=jnp.bfloat16):
    result = spread * jax.random.normal(rng, extent, jnp.float32)
    if cuts:
        result = result * steps_of(rng, extent, cuts, -0.22, 0.18)
    return jnp.clip(result, -limit, limit).astype(kind)


def setup_inputs(seed: int = 0, part: int = 0) -> dict:
    key_of = jax.random.split(jax.random.key(seed), 6)
    own_keys = jax.random.split(jax.random.fold_in(key_of[5], part), 6)
    queries = draw_queries(jax.random.fold_in(jax.random.fold_in(key_of[5], part), 71), part)
    keys = draw_keys(jax.random.fold_in(jax.random.fold_in(key_of[5], part), 71), part)
    values = noise(own_keys[2], (TOKENS, WIDTH), 1.0, 6.0, ((0, 16),))
    out_grad = noise(own_keys[3], (TOKENS, WIDTH), 1.0, 6.0, ((0, 16),))
    conv_weight = noise(key_of[4], (STRIDE, HEADS), STRIDE ** -0.5, 2.0, (), jnp.float32)
    return dict(queries=queries, keys=keys, values=values, out_grad=out_grad, conv_weight=conv_weight)


def compress(rows, conv_weight):
    count = rows.shape[0]
    shaped = rows.reshape(count // STRIDE, STRIDE, HEADS, HEAD_DIM).astype(jnp.float32)
    return jnp.einsum('cshd,sh->chd', shaped, conv_weight).astype(jnp.bfloat16)


def reference(queries, keys, values, out_grad, conv_weight):
    scale = HEAD_DIM ** -0.5
    mem_keys = compress(keys, conv_weight).astype(jnp.float32)
    mem_vals = compress(values, conv_weight).astype(jnp.float32)
    total_mem = mem_keys.shape[0]
    owner = jnp.arange(total_mem, dtype=jnp.int32) // MEM_ROWS
    causal = jnp.arange(TOK_DEV)[:, None] >= jnp.arange(TOK_DEV)[None, :]

    def shard(carry, index):
        dmk, dmv = carry
        start = index * TOK_DEV
        q3 = lax.dynamic_slice_in_dim(queries, start, TOK_DEV, 0).reshape(TOK_DEV, HEADS, HEAD_DIM).astype(jnp.float32)
        k3 = lax.dynamic_slice_in_dim(keys, start, TOK_DEV, 0).reshape(TOK_DEV, HEADS, HEAD_DIM).astype(jnp.float32)
        v3 = lax.dynamic_slice_in_dim(values, start, TOK_DEV, 0).reshape(TOK_DEV, HEADS, HEAD_DIM).astype(jnp.float32)
        g3 = lax.dynamic_slice_in_dim(out_grad, start, TOK_DEV, 0).reshape(TOK_DEV, HEADS, HEAD_DIM).astype(jnp.float32)
        valid = owner < index
        sm = jnp.einsum('shd,nhd->hsn', q3, mem_keys) * scale
        sl = jnp.einsum('shd,thd->hst', q3, k3) * scale
        sm = jnp.where(valid[None, None, :], sm, -1e30)
        sl = jnp.where(causal[None], sl, -1e30)
        high = jnp.maximum(sm.max(-1), sl.max(-1))
        total = jnp.sum(jnp.where(valid[None, None, :], jnp.exp(sm - high[..., None]), 0.0), -1)
        total = total + jnp.sum(jnp.where(causal[None], jnp.exp(sl - high[..., None]), 0.0), -1)
        lse = high + jnp.log(total)
        pm = jnp.where(valid[None, None, :], jnp.exp(sm - lse[..., None]), 0.0)
        pl = jnp.where(causal[None], jnp.exp(sl - lse[..., None]), 0.0)
        out = jnp.einsum('hsn,nhd->hsd', pm, mem_vals) + jnp.einsum('hst,thd->hsd', pl, v3)
        dsum = jnp.einsum('hsd,shd->hs', out, g3)
        pmb = pm.astype(jnp.bfloat16).astype(jnp.float32)
        plb = pl.astype(jnp.bfloat16).astype(jnp.float32)
        dpm = jnp.einsum('shd,nhd->hsn', g3, mem_vals)
        dpl = jnp.einsum('shd,thd->hst', g3, v3)
        dsm = (pm * (dpm - dsum[..., None])).astype(jnp.bfloat16).astype(jnp.float32)
        dsl = (pl * (dpl - dsum[..., None])).astype(jnp.bfloat16).astype(jnp.float32)
        dq3 = (jnp.einsum('hsn,nhd->shd', dsm, mem_keys) + jnp.einsum('hst,thd->shd', dsl, k3)) * scale
        dk3 = jnp.einsum('hst,shd->thd', dsl, q3) * scale
        dv3 = jnp.einsum('hst,shd->thd', plb, g3)
        dmk = dmk + jnp.einsum('hsn,shd->nhd', dsm, q3) * scale
        dmv = dmv + jnp.einsum('hsn,shd->nhd', pmb, g3)
        return (dmk, dmv), (dq3, dk3, dv3)

    zeros = jnp.zeros((total_mem, HEADS, HEAD_DIM), jnp.float32)
    (dmk, dmv), (dq3, dk3, dv3) = lax.scan(shard, (zeros, zeros), jnp.arange(N_CTX, dtype=jnp.int32))
    spread_k = jnp.einsum('chd,sh->cshd', dmk, conv_weight).reshape(TOKENS, HEADS, HEAD_DIM)
    spread_v = jnp.einsum('chd,sh->cshd', dmv, conv_weight).reshape(TOKENS, HEADS, HEAD_DIM)
    dq = dq3.reshape(TOKENS, WIDTH).astype(jnp.bfloat16)
    dk = (dk3.reshape(TOKENS, HEADS, HEAD_DIM) + spread_k).reshape(TOKENS, WIDTH).astype(jnp.bfloat16)
    dv = (dv3.reshape(TOKENS, HEADS, HEAD_DIM) + spread_v).reshape(TOKENS, WIDTH).astype(jnp.bfloat16)
    key_rows = keys.reshape(total_mem, STRIDE, HEADS, HEAD_DIM).astype(jnp.float32)
    val_rows = values.reshape(total_mem, STRIDE, HEADS, HEAD_DIM).astype(jnp.float32)
    dconv = jnp.einsum('chd,cshd->sh', dmk, key_rows) + jnp.einsum('chd,cshd->sh', dmv, val_rows)
    return (dq, dk, dv, dconv)
```

```python
import functools

import jax
import jax.numpy as jnp
from jax import lax
from jax.experimental import pallas as pl
from jax.experimental.pallas import tpu as pltpu
from jax.sharding import PartitionSpec as P

MESH = pl.DeviceIdType.MESH
F32 = jnp.float32
BF16 = jnp.bfloat16
LAYER = 4
HEADS_PER_STEP = 2


def dot(a, b, ca, cb):
    return lax.dot_general(a, b, (((ca,), (cb,)), ((), ())), preferred_element_type=F32)


def kernel(
    n, q_ref, k_ref, v_ref, g_ref, cw_ref, dq_ref, dk_ref, dv_ref, dc_ref,
    mem, part, cbuf, ybuf, zbuf, dbuf, wexp, dkl, dvl,
    az_s, az_r, ay_s, ay_r, ac_s, ac_r,
    rc_s, rc_r, ry_s, ry_r, rz_s, rz_r, d_s, d_r,
):
    count, width = q_ref.shape
    stride, heads = cw_ref.shape
    dim = width // heads
    rows = count // stride
    layers = n // LAYER
    total = rows * n
    scale = dim ** (-0.5)
    me = lax.axis_index("ctx")
    z = me // LAYER
    r = me % LAYER
    y = r // 2
    c = r % 2
    base = z * LAYER
    core_peer = base + y * 2 + (1 - c)
    y_peer = base + (1 - y) * 2 + c

    barrier = pltpu.get_barrier_semaphore()

    def greet(i, carry):
        pl.semaphore_signal(
            barrier, inc=1, device_id={"ctx": (me + i) % n}, device_id_type=MESH
        )
        return carry

    lax.fori_loop(1, n, greet, 0)

    def block(ref, owner):
        return ref.at[:, pl.ds(pl.multiple_of(owner * rows, rows), rows), :]

    def lanes(h):
        return pl.ds(pl.multiple_of(h * dim, dim), dim)

    def remote(src, dst, send, recv, dev):
        return pltpu.make_async_remote_copy(
            src_ref=src, dst_ref=dst, send_sem=send, recv_sem=recv,
            device_id={"ctx": dev}, device_id_type=MESH,
        )

    for h in range(heads):
        wexp[:, h * dim:(h + 1) * dim] = jnp.broadcast_to(cw_ref[:, h:h + 1], (stride, dim))

    my_rows = pl.ds(pl.multiple_of(me * rows, rows), rows)

    def compress(h, carry):
        w = wexp[:, lanes(h)][None]
        for i, src in enumerate((k_ref, v_ref)):
            x = src[:, lanes(h)].astype(F32).reshape(rows, stride, dim)
            mem[i, my_rows, lanes(h)] = (x * w).sum(axis=1).astype(BF16)
        return carry

    lax.fori_loop(0, heads, compress, 0)
    pl.semaphore_wait(barrier, n - 1)

    def gather_z(to, sender):
        own = block(mem, sender * LAYER + r)
        return remote(own, own, az_s.at[to], az_r.at[sender], to * LAYER + r)

    def gather_y(zs, yy):
        b = block(mem, zs * LAYER + yy * 2 + c)
        return remote(b, b, ay_s.at[zs], ay_r.at[zs], y_peer)

    def gather_c(zs, yy, cc):
        b = block(mem, zs * LAYER + yy * 2 + cc)
        return remote(b, b, ac_s.at[zs, yy], ac_r.at[zs, yy], core_peer)

    def each(lo, hi, fn):
        def step(i, carry):
            fn(i)
            return carry
        lax.fori_loop(lo, hi, step, 0)

    each(0, layers - 1 - z, lambda i: gather_z(layers - 1 - i, z).start())
    gather_y(z, y).start()
    gather_c(z, y, c).start()

    def clear(zs):
        span = pl.ds(pl.multiple_of(zs * LAYER * rows, LAYER * rows), LAYER * rows)
        mem[:, span, :] = jnp.zeros((2, LAYER * rows, width), BF16)

    each(z + 1, layers, clear)

    def arrive_z(i):
        zs = z - i
        gather_z(z, zs).wait_recv()
        gather_y(zs, y).start()
        gather_c(zs, y, c).start()

    def arrive_y(i):
        zs = z - i
        gather_y(zs, 1 - y).wait_recv()
        gather_c(zs, 1 - y, c).start()

    def arrive_c(i):
        zs = z - i
        gather_c(zs, y, 1 - c).wait_recv()
        gather_c(zs, 1 - y, 1 - c).wait_recv()

    each(1, z + 1, arrive_z)
    each(0, z + 1, arrive_y)
    each(0, z + 1, arrive_c)

    valid = lax.broadcasted_iota(jnp.int32, (total, count), 0) < me * rows
    causal = lax.broadcasted_iota(jnp.int32, (count, count), 0) <= lax.broadcasted_iota(
        jnp.int32, (count, count), 1
    )

    def one_head(h):
        q, k, v, g = (x[:, lanes(h)] for x in (q_ref, k_ref, v_ref, g_ref))
        mk, mv = mem[0, :, lanes(h)], mem[1, :, lanes(h)]
        sm = jnp.where(valid, dot(mk, q, 1, 1) * scale, -1e30)
        sl = jnp.where(causal, dot(k, q, 1, 1) * scale, -1e30)
        dpm, dpl = dot(mv, g, 1, 1), dot(v, g, 1, 1)
        high = jnp.maximum(sm.max(0, keepdims=True), sl.max(0, keepdims=True))
        em, el = jnp.exp(sm - high), jnp.exp(sl - high)
        inv = 1.0 / (em.sum(0, keepdims=True) + el.sum(0, keepdims=True))
        pm, plo = em * inv, el * inv
        dsum = (pm * dpm).sum(0, keepdims=True) + (plo * dpl).sum(0, keepdims=True)
        dsm = (pm * (dpm - dsum)).astype(BF16)
        dsl = (plo * (dpl - dsum)).astype(BF16)
        dq = (dot(dsm, mk, 0, 0) + dot(dsl, k, 0, 0)) * scale
        pk = dot(dsm, q, 1, 0) * scale
        pv = dot(pm.astype(BF16), g, 1, 0)
        lk = dot(dsl, q, 1, 0) * scale
        lv = dot(plo.astype(BF16), g, 1, 0)
        return dq.astype(BF16), pk.astype(BF16), pv.astype(BF16), lk, lv

    def head_step(i):
        hs = [i * HEADS_PER_STEP + j for j in range(HEADS_PER_STEP)]
        for h, (dq, pk, pv, lk, lv) in zip(hs, [one_head(h) for h in hs]):
            dq_ref[:, lanes(h)] = dq
            part[0, :, lanes(h)] = pk
            part[1, :, lanes(h)] = pv
            dkl[:, lanes(h)] = lk
            dvl[:, lanes(h)] = lv

    each(0, heads // HEADS_PER_STEP, head_step)

    def reduce_c(zs, yy, cc):
        return remote(
            block(part, zs * LAYER + yy * 2 + cc), cbuf.at[zs * 2 + yy],
            rc_s.at[zs, yy], rc_r.at[zs, yy], core_peer,
        )

    def reduce_y(zs, yy):
        return remote(
            block(part, zs * LAYER + yy * 2 + c), ybuf.at[zs], ry_s.at[zs], ry_r.at[zs], y_peer
        )

    def reduce_z(to, sender):
        return remote(
            block(part, to * LAYER + r), zbuf.at[sender], rz_s.at[to], rz_r.at[sender],
            to * LAYER + r,
        )

    def send_c(zs):
        reduce_c(zs, 1 - y, 1 - c).start()
        reduce_c(zs, y, 1 - c).start()

    each(0, z + 1, send_c)

    def add_into(owner, other):
        b = block(part, owner)
        b[...] = (b[...].astype(F32) + other[...].astype(F32)).astype(BF16)

    def sum_c(zs):
        reduce_c(zs, 1 - y, c).wait_recv()
        add_into(zs * LAYER + (1 - y) * 2 + c, cbuf.at[zs * 2 + 1 - y])
        reduce_y(zs, 1 - y).start()
        reduce_c(zs, y, c).wait_recv()
        add_into(zs * LAYER + r, cbuf.at[zs * 2 + y])

    each(0, z + 1, sum_c)

    def sum_y(zs):
        reduce_y(zs, y).wait_recv()
        add_into(zs * LAYER + r, ybuf.at[zs])

        @pl.when(zs < z)
        def _():
            reduce_z(zs, z).start()

    each(0, z + 1, sum_y)

    zbuf[z] = part[:, my_rows, :]
    each(z + 1, layers, lambda zz: reduce_z(z, zz).wait_recv())

    def clear_z(zz):
        zbuf[zz] = jnp.zeros((2, rows, width), BF16)

    each(0, z, clear_z)

    lane = lax.broadcasted_iota(jnp.int32, (stride, dbuf.shape[-1]), 1)

    def conv_head(h, acc):
        t = jnp.zeros((stride, dim), F32)
        for i, (src, loc, out) in enumerate(((k_ref, dkl, dk_ref), (v_ref, dvl, dv_ref))):
            x = src[:, lanes(h)].astype(F32).reshape(rows, stride, dim)
            d = zbuf[:, i, :, lanes(h)].astype(F32).sum(axis=0)[:, None, :]
            t += (x * d).sum(axis=0)
            spread = (d * wexp[:, lanes(h)][None]).reshape(count, dim)
            out[:, lanes(h)] = (loc[:, lanes(h)] + spread).astype(BF16)
        return jnp.where(lane == h, t.sum(axis=1, keepdims=True), acc)

    dbuf[me] = lax.fori_loop(0, heads, conv_head, jnp.zeros(lane.shape, F32))

    def conv_copy(to, sender):
        return remote(dbuf.at[sender], dbuf.at[sender], d_s.at[to], d_r.at[sender], to)

    each(1, n, lambda i: conv_copy((me + i) % n, me).start())

    each(z + 1, layers, lambda to: gather_z(to, z).wait_send())

    def ended(zs):
        gather_y(zs, y).wait_send()
        gather_c(zs, y, c).wait_send()
        gather_c(zs, 1 - y, c).wait_send()
        reduce_c(zs, 0, 1 - c).wait_send()
        reduce_c(zs, 1, 1 - c).wait_send()
        reduce_y(zs, 1 - y).wait_send()

    each(0, z + 1, ended)
    each(0, z, lambda zs: reduce_z(zs, z).wait_send())
    each(1, n, lambda i: conv_copy(me, (me + i) % n).wait_recv())
    dc_ref[...] = dbuf[...].sum(axis=0)[:, :heads]
    each(1, n, lambda i: conv_copy((me + i) % n, me).wait_send())


def local(n, queries, keys, values, out_grad, conv_weight):
    count, width = queries.shape
    stride, heads = conv_weight.shape
    rows = count // stride
    layers = n // LAYER
    big = jax.ShapeDtypeStruct((count, width), BF16)
    vmem = pl.BlockSpec(memory_space=pltpu.VMEM)
    dma = pltpu.SemaphoreType.DMA
    return pl.pallas_call(
        functools.partial(kernel, n),
        out_shape=(big, big, big, jax.ShapeDtypeStruct((stride, heads), F32)),
        in_specs=[vmem] * 5,
        out_specs=[vmem] * 4,
        scratch_shapes=[
            pltpu.VMEM((2, rows * n, width), BF16),
            pltpu.VMEM((2, rows * n, width), BF16),
            pltpu.VMEM((layers * 2, 2, rows, width), BF16),
            pltpu.VMEM((layers, 2, rows, width), BF16),
            pltpu.VMEM((layers, 2, rows, width), BF16),
            pltpu.VMEM((n, stride, 128 * pl.cdiv(heads, 128)), F32),
            pltpu.VMEM((stride, width), F32),
            pltpu.VMEM((count, width), F32),
            pltpu.VMEM((count, width), F32),
            dma((layers,)), dma((layers,)), dma((layers,)), dma((layers,)),
            dma((layers, 2)), dma((layers, 2)),
            dma((layers, 2)), dma((layers, 2)),
            dma((layers,)), dma((layers,)), dma((layers,)), dma((layers,)),
            dma((n,)), dma((n,)),
        ],
        compiler_params=pltpu.CompilerParams(
            collective_id=0, has_side_effects=True, vmem_limit_bytes=60 * 2**20
        ),
    )(queries, keys, values, out_grad, conv_weight)


def solution(mesh):
    rows = P(("groups", "ctx"), None)
    return jax.shard_map(
        functools.partial(local, mesh.shape["ctx"]),
        mesh=mesh,
        in_specs=(rows, rows, rows, rows, P()),
        out_specs=(rows, rows, rows, P("groups", None)),
        check_vma=False,
    )
```

```python
import functools

import jax
import jax.numpy as jnp
from jax import lax
from jax.experimental import pallas as pl
from jax.experimental.pallas import tpu as pltpu
from jax.sharding import PartitionSpec as P

MESH = pl.DeviceIdType.MESH
F32 = jnp.float32
BF16 = jnp.bfloat16
LAYER = 4
HEADS_PER_STEP = 2
GROUPS = 4


def dot(a, b, ca, cb):
    return lax.dot_general(a, b, (((ca,), (cb,)), ((), ())), preferred_element_type=F32)


def kernel(
    n, q_ref, k_ref, v_ref, g_ref, cw_ref, dq_ref, dk_ref, dv_ref, dc_ref,
    mem, part, cbuf, ybuf, zbuf, dbuf, wexp, dkl, dvl,
    az_s, az_r, ay_s, ay_r, ac_s, ac_r,
    rc_s, rc_r, ry_s, ry_r, rz_s, rz_r, d_s, d_r,
):
    count, width = q_ref.shape
    stride, heads = cw_ref.shape
    dim = width // heads
    rows = count // stride
    layers = n // LAYER
    total = rows * n
    scale = dim ** (-0.5)
    me = lax.axis_index("ctx")
    z = me // LAYER
    r = me % LAYER
    y = r // 2
    c = r % 2
    base = z * LAYER
    core_peer = base + y * 2 + (1 - c)
    y_peer = base + (1 - y) * 2 + c

    barrier = pltpu.get_barrier_semaphore()

    def greet(i, carry):
        pl.semaphore_signal(
            barrier, inc=1, device_id={"ctx": (me + i) % n}, device_id_type=MESH
        )
        return carry

    lax.fori_loop(1, n, greet, 0)

    part_width = width // GROUPS

    def cols(gi):
        return pl.ds(gi * part_width, part_width)

    def block(ref, owner, gi):
        return ref.at[:, pl.ds(pl.multiple_of(owner * rows, rows), rows), cols(gi)]

    def lanes(h):
        return pl.ds(pl.multiple_of(h * dim, dim), dim)

    def remote(src, dst, send, recv, dev):
        return pltpu.make_async_remote_copy(
            src_ref=src, dst_ref=dst, send_sem=send, recv_sem=recv,
            device_id={"ctx": dev}, device_id_type=MESH,
        )

    for h in range(heads):
        wexp[:, h * dim:(h + 1) * dim] = jnp.broadcast_to(cw_ref[:, h:h + 1], (stride, dim))

    my_rows = pl.ds(pl.multiple_of(me * rows, rows), rows)

    def compress(h, carry):
        w = wexp[:, lanes(h)][None]
        for i, src in enumerate((k_ref, v_ref)):
            x = src[:, lanes(h)].astype(F32).reshape(rows, stride, dim)
            mem[i, my_rows, lanes(h)] = (x * w).sum(axis=1).astype(BF16)
        return carry

    lax.fori_loop(0, heads, compress, 0)
    pl.semaphore_wait(barrier, n - 1)

    def gather_z(gi, to, sender):
        own = block(mem, sender * LAYER + r, gi)
        return remote(own, own, az_s.at[gi, to], az_r.at[gi, sender], to * LAYER + r)

    def gather_y(gi, zs, yy):
        b = block(mem, zs * LAYER + yy * 2 + c, gi)
        return remote(b, b, ay_s.at[gi, zs], ay_r.at[gi, zs], y_peer)

    def gather_c(gi, zs, yy, cc):
        b = block(mem, zs * LAYER + yy * 2 + cc, gi)
        return remote(b, b, ac_s.at[gi, zs, yy], ac_r.at[gi, zs, yy], core_peer)

    def each(lo, hi, fn):
        def step(i, carry):
            fn(i)
            return carry
        lax.fori_loop(lo, hi, step, 0)

    for gi in range(GROUPS):
        each(0, layers - 1 - z, lambda i: gather_z(gi, layers - 1 - i, z).start())
        gather_y(gi, z, y).start()
        gather_c(gi, z, y, c).start()

    def clear(zs):
        span = pl.ds(pl.multiple_of(zs * LAYER * rows, LAYER * rows), LAYER * rows)
        mem[:, span, :] = jnp.zeros((2, LAYER * rows, width), BF16)

    each(z + 1, layers, clear)

    def arrive_z(gi, i):
        zs = z - i
        gather_z(gi, z, zs).wait_recv()
        gather_y(gi, zs, y).start()
        gather_c(gi, zs, y, c).start()

    def arrive_y(gi, i):
        zs = z - i
        gather_y(gi, zs, 1 - y).wait_recv()
        gather_c(gi, zs, 1 - y, c).start()

    def arrive_c(gi, i):
        zs = z - i
        gather_c(gi, zs, y, 1 - c).wait_recv()
        gather_c(gi, zs, 1 - y, 1 - c).wait_recv()

    valid = lax.broadcasted_iota(jnp.int32, (total, count), 0) < me * rows
    causal = lax.broadcasted_iota(jnp.int32, (count, count), 0) <= lax.broadcasted_iota(
        jnp.int32, (count, count), 1
    )

    def one_head(h):
        q, k, v, g = (x[:, lanes(h)] for x in (q_ref, k_ref, v_ref, g_ref))
        mk, mv = mem[0, :, lanes(h)], mem[1, :, lanes(h)]
        sm = jnp.where(valid, dot(mk, q, 1, 1) * scale, -1e30)
        sl = jnp.where(causal, dot(k, q, 1, 1) * scale, -1e30)
        dpm, dpl = dot(mv, g, 1, 1), dot(v, g, 1, 1)
        high = jnp.maximum(sm.max(0, keepdims=True), sl.max(0, keepdims=True))
        em, el = jnp.exp(sm - high), jnp.exp(sl - high)
        inv = 1.0 / (em.sum(0, keepdims=True) + el.sum(0, keepdims=True))
        pm, plo = em * inv, el * inv
        dsum = (pm * dpm).sum(0, keepdims=True) + (plo * dpl).sum(0, keepdims=True)
        dsm = (pm * (dpm - dsum)).astype(BF16)
        dsl = (plo * (dpl - dsum)).astype(BF16)
        dq = (dot(dsm, mk, 0, 0) + dot(dsl, k, 0, 0)) * scale
        pk = dot(dsm, q, 1, 0) * scale
        pv = dot(pm.astype(BF16), g, 1, 0)
        lk = dot(dsl, q, 1, 0) * scale
        lv = dot(plo.astype(BF16), g, 1, 0)
        return dq.astype(BF16), pk.astype(BF16), pv.astype(BF16), lk, lv

    def head_step(i):
        hs = [i * HEADS_PER_STEP + j for j in range(HEADS_PER_STEP)]
        for h, (dq, pk, pv, lk, lv) in zip(hs, [one_head(h) for h in hs]):
            dq_ref[:, lanes(h)] = dq
            part[0, :, lanes(h)] = pk
            part[1, :, lanes(h)] = pv
            dkl[:, lanes(h)] = lk
            dvl[:, lanes(h)] = lv

    steps = heads // HEADS_PER_STEP // GROUPS

    def reduce_c(gi, zs, yy, cc):
        return remote(
            block(part, zs * LAYER + yy * 2 + cc, gi), cbuf.at[zs * 2 + yy, :, :, cols(gi)],
            rc_s.at[gi, zs, yy], rc_r.at[gi, zs, yy], core_peer,
        )

    def reduce_y(gi, zs, yy):
        return remote(
            block(part, zs * LAYER + yy * 2 + c, gi), ybuf.at[zs, :, :, cols(gi)],
            ry_s.at[gi, zs], ry_r.at[gi, zs], y_peer,
        )

    def reduce_z(gi, to, sender):
        return remote(
            block(part, to * LAYER + r, gi), zbuf.at[sender, :, :, cols(gi)],
            rz_s.at[gi, to], rz_r.at[gi, sender], to * LAYER + r,
        )

    def send_c(gi, zs):
        reduce_c(gi, zs, 1 - y, 1 - c).start()
        reduce_c(gi, zs, y, 1 - c).start()

    def add_into(gi, owner, other):
        b = block(part, owner, gi)
        b[...] = (b[...].astype(F32) + other[...].astype(F32)).astype(BF16)

    def sum_c(gi, zs):
        reduce_c(gi, zs, 1 - y, c).wait_recv()
        add_into(gi, zs * LAYER + (1 - y) * 2 + c, cbuf.at[zs * 2 + 1 - y, :, :, cols(gi)])
        reduce_y(gi, zs, 1 - y).start()
        reduce_c(gi, zs, y, c).wait_recv()
        add_into(gi, zs * LAYER + r, cbuf.at[zs * 2 + y, :, :, cols(gi)])

    def sum_y(gi, zs):
        reduce_y(gi, zs, y).wait_recv()
        add_into(gi, zs * LAYER + r, ybuf.at[zs, :, :, cols(gi)])

        @pl.when(zs < z)
        def _():
            reduce_z(gi, zs, z).start()

    for s in range(GROUPS + 4):
        if s < GROUPS:
            each(1, z + 1, functools.partial(arrive_z, s))
        if 0 <= s - 1 < GROUPS:
            each(0, z + 1, functools.partial(arrive_y, s - 1))
        if 0 <= s - 2 < GROUPS:
            each(0, z + 1, functools.partial(arrive_c, s - 2))
            each((s - 2) * steps, (s - 1) * steps, head_step)
            each(0, z + 1, functools.partial(send_c, s - 2))
        if 0 <= s - 3 < GROUPS:
            each(0, z + 1, functools.partial(sum_c, s - 3))
        if 0 <= s - 4 < GROUPS:
            each(0, z + 1, functools.partial(sum_y, s - 4))

    zbuf[z] = part[:, my_rows, :]
    for gi in range(GROUPS):
        each(z + 1, layers, lambda zz: reduce_z(gi, z, zz).wait_recv())

    def clear_z(zz):
        zbuf[zz] = jnp.zeros((2, rows, width), BF16)

    each(0, z, clear_z)

    lane = lax.broadcasted_iota(jnp.int32, (stride, dbuf.shape[-1]), 1)

    def conv_head(h, acc):
        t = jnp.zeros((stride, dim), F32)
        for i, (src, loc, out) in enumerate(((k_ref, dkl, dk_ref), (v_ref, dvl, dv_ref))):
            x = src[:, lanes(h)].astype(F32).reshape(rows, stride, dim)
            d = zbuf[:, i, :, lanes(h)].astype(F32).sum(axis=0)[:, None, :]
            t += (x * d).sum(axis=0)
            spread = (d * wexp[:, lanes(h)][None]).reshape(count, dim)
            out[:, lanes(h)] = (loc[:, lanes(h)] + spread).astype(BF16)
        return jnp.where(lane == h, t.sum(axis=1, keepdims=True), acc)

    dbuf[me] = lax.fori_loop(0, heads, conv_head, jnp.zeros(lane.shape, F32))

    def conv_copy(to, sender):
        return remote(dbuf.at[sender], dbuf.at[sender], d_s.at[to], d_r.at[sender], to)

    each(1, n, lambda i: conv_copy((me + i) % n, me).start())

    def ended(gi, zs):
        gather_y(gi, zs, y).wait_send()
        gather_c(gi, zs, y, c).wait_send()
        gather_c(gi, zs, 1 - y, c).wait_send()
        reduce_c(gi, zs, 0, 1 - c).wait_send()
        reduce_c(gi, zs, 1, 1 - c).wait_send()
        reduce_y(gi, zs, 1 - y).wait_send()

    for gi in range(GROUPS):
        each(z + 1, layers, lambda to: gather_z(gi, to, z).wait_send())
        each(0, z + 1, functools.partial(ended, gi))
        each(0, z, lambda zs: reduce_z(gi, zs, z).wait_send())
    each(1, n, lambda i: conv_copy(me, (me + i) % n).wait_recv())
    dc_ref[...] = dbuf[...].sum(axis=0)[:, :heads]
    each(1, n, lambda i: conv_copy((me + i) % n, me).wait_send())


def local(n, queries, keys, values, out_grad, conv_weight):
    count, width = queries.shape
    stride, heads = conv_weight.shape
    rows = count // stride
    layers = n // LAYER
    big = jax.ShapeDtypeStruct((count, width), BF16)
    vmem = pl.BlockSpec(memory_space=pltpu.VMEM)
    dma = pltpu.SemaphoreType.DMA
    return pl.pallas_call(
        functools.partial(kernel, n),
        out_shape=(big, big, big, jax.ShapeDtypeStruct((stride, heads), F32)),
        in_specs=[vmem] * 5,
        out_specs=[vmem] * 4,
        scratch_shapes=[
            pltpu.VMEM((2, rows * n, width), BF16),
            pltpu.VMEM((2, rows * n, width), BF16),
            pltpu.VMEM((layers * 2, 2, rows, width), BF16),
            pltpu.VMEM((layers, 2, rows, width), BF16),
            pltpu.VMEM((layers, 2, rows, width), BF16),
            pltpu.VMEM((n, stride, 128 * pl.cdiv(heads, 128)), F32),
            pltpu.VMEM((stride, width), F32),
            pltpu.VMEM((count, width), F32),
            pltpu.VMEM((count, width), F32),
            dma((GROUPS, layers,)), dma((GROUPS, layers,)), dma((GROUPS, layers,)), dma((GROUPS, layers,)),
            dma((GROUPS, layers, 2)), dma((GROUPS, layers, 2)),
            dma((GROUPS, layers, 2)), dma((GROUPS, layers, 2)),
            dma((GROUPS, layers,)), dma((GROUPS, layers,)), dma((GROUPS, layers,)), dma((GROUPS, layers,)),
            dma((n,)), dma((n,)),
        ],
        compiler_params=pltpu.CompilerParams(
            collective_id=0, has_side_effects=True, vmem_limit_bytes=60 * 2**20
        ),
    )(queries, keys, values, out_grad, conv_weight)


def solution(mesh):
    rows = P(("groups", "ctx"), None)
    return jax.shard_map(
        functools.partial(local, mesh.shape["ctx"]),
        mesh=mesh,
        in_specs=(rows, rows, rows, rows, P()),
        out_specs=(rows, rows, rows, P("groups", None)),
        check_vma=False,
    )
```
